512 devices in a mesh: energy: 32 (over x, z_hi, core), cuts: 16 (over z_lo, y).
Axes of the slice: x: 4, y: 8, z: 8 (z_hi: 4, z_lo: 2; z = z_hi * 2 + z_lo), core: 2. Of those that a mesh axis runs over, the one named last changes fastest.
Arguments:
- green_diag: bfloat16 [16, 128, 2, 256, 256], P('cuts', 'energy'), may hold values from -0.375 to 0.375
- green_upper: bfloat16 [16, 128, 2, 256, 256], P('cuts', 'energy'), may hold values from -0.375 to 0.375
- sigma_lesser: bfloat16 [16, 128, 2, 256, 256], P('cuts', 'energy'), may hold values from -6 to 6
- screening: bfloat16 [16, 128, 2, 256, 256], P('cuts', 'energy'), may hold values from -0.375 to 0.375
Outputs:
- polar_screened: bfloat16 [16, 128, 2, 256, 256], P('cuts', 'energy')
The draws below stay inside these ranges and needn't reach their ends.
All inputs are finite; a program needn't handle non-finite values.
Results may differ from the reference program's by a relative error of at most 0.013.
Values may be sent and summed in bfloat16 or wider, within the bound.
No kernel may reach another device: no remote copies, remote signals or barrier semaphores. Data moves between devices by JAX's collectives and lax.ppermute only.
A program may use at most 64 MiB of HBM per device.

```python
import jax
import jax.numpy as jnp
from jax import lax

B = 256
NE = 128
SLICES = 16
PAD = 256


def shard_levels(own_key, dims, cuts, least, top_value):
    def one(dim, blocks):
        steps = jax.random.uniform(jax.random.fold_in(jax.random.fold_in(own_key, 6), dim), (blocks,), jnp.float32, least / len(cuts), top_value / len(cuts))
        return jnp.repeat(jnp.exp(steps), dims[dim] // blocks).reshape((-1,) + (1,) * (len(dims) - dim - 1))

    loudness = one(*cuts[0])
    for cut in cuts[1:]:
        loudness = loudness * one(*cut)
    return loudness


def centred(rng, extent, spread, most, split=(), dtype=jnp.bfloat16):
    gain = shard_levels(rng, extent, split, -0.22, 0.18) if split else 1.0
    array = jax.random.normal(rng, extent, jnp.float32) * spread * gain
    return jnp.minimum(jnp.maximum(array, -most), most).astype(dtype)


def setup_inputs(seed: int = 0) -> dict:
    arg_keys = jax.random.split(jax.random.key(seed), 5)
    return {
        "green_diag": centred(arg_keys[0], (SLICES, NE, 2, B, B), B ** -0.5, 0.375, ((0, 16), (1, 32))),
        "green_upper": centred(arg_keys[1], (SLICES, NE, 2, B, B), B ** -0.5, 0.375, ((0, 16), (1, 32))),
        "sigma_lesser": centred(arg_keys[2], (SLICES, NE, 2, B, B), 1.0, 6.0, ((0, 16), (1, 32))),
        "screening": centred(arg_keys[3], (SLICES, NE, 2, B, B), B ** -0.5, 0.375, ((0, 16), (1, 32))),
    }


def times_block(left, right):
    left = left.astype(jnp.float32)
    right = right.astype(jnp.float32)
    real = jnp.einsum('eij,ejk->eik', left[:, 0], right[:, 0]) - jnp.einsum('eij,ejk->eik', left[:, 1], right[:, 1])
    imag = jnp.einsum('eij,ejk->eik', left[:, 0], right[:, 1]) + jnp.einsum('eij,ejk->eik', left[:, 1], right[:, 0])
    return jnp.stack([real, imag], axis=1)


def times_adjoint(left, right):
    left = left.astype(jnp.float32)
    right = right.astype(jnp.float32)
    real = jnp.einsum('eij,ekj->eik', left[:, 0], right[:, 0]) + jnp.einsum('eij,ekj->eik', left[:, 1], right[:, 1])
    imag = jnp.einsum('eij,ekj->eik', left[:, 1], right[:, 0]) - jnp.einsum('eij,ekj->eik', left[:, 0], right[:, 1])
    return jnp.stack([real, imag], axis=1)


def one_slice(inputs):
    green_diag, green_upper, sigma_here, sigma_after, screening = inputs
    own_term = times_block(green_diag, sigma_here).astype(jnp.bfloat16)
    pair_term = times_block(green_upper, sigma_after).astype(jnp.bfloat16)
    lesser = (times_adjoint(own_term, green_diag) + times_adjoint(pair_term, green_upper)).astype(jnp.bfloat16)
    values = lesser.astype(jnp.float32)
    signal = lax.complex(values[:, 0], values[:, 1])
    spectrum = jnp.fft.fft(signal, n=PAD, axis=0)
    power = jnp.real(spectrum) ** 2 + jnp.imag(spectrum) ** 2
    lagged = jnp.fft.ifft(power, axis=0)[:NE]
    polar = (jnp.stack([jnp.real(lagged), jnp.imag(lagged)], axis=1) / NE).astype(jnp.bfloat16)
    screened_left = times_block(screening, polar).astype(jnp.bfloat16)
    return times_adjoint(screened_left, screening).astype(jnp.bfloat16)


def reference(green_diag, green_upper, sigma_lesser, screening):
    sigma_next = jnp.concatenate([sigma_lesser[1:], jnp.zeros_like(sigma_lesser[:1])], axis=0)
    return lax.map(one_slice, (green_diag, green_upper, sigma_lesser, sigma_next, screening))
```

```python
import functools
import math

import jax
import jax.numpy as jnp
import numpy as np
from jax import lax
from jax.experimental import pallas as pl
from jax.experimental.pallas import tpu as pltpu
from jax.sharding import PartitionSpec as P


F32 = jnp.float32
BF16 = jnp.bfloat16
FIRST = 1


def shifted(value, axis, steps):
    count = lax.axis_size(axis)
    leading, last = (max(0, -steps), min(count, count - steps))
    return lax.ppermute(value, axis, [(source, source + steps) for source in range(leading, last)])


def product(left, right):
    rows = left.shape[0] // 2
    by_real = jnp.dot(left, right[0], preferred_element_type=F32)
    by_imag = jnp.dot(left, right[1], preferred_element_type=F32)
    return by_real[:rows] - by_imag[rows:], by_real[rows:] + by_imag[:rows]


def product_adjoint(left, right):
    rows = left.shape[0] // 2
    turned = functools.partial(
        lax.dot_general, dimension_numbers=(((1,), (1,)), ((), ())), preferred_element_type=F32
    )
    by_real = turned(left, right[0])
    by_imag = turned(left, right[1])
    return by_real[:rows] + by_imag[rows:], by_real[rows:] - by_imag[:rows]


def stacked(ref):
    return ref[0, 0].reshape(-1, ref.shape[-1])


def joined(pair):
    return jnp.concatenate([part.astype(BF16) for part in pair], axis=0)


def own_kernel(green, sigma, out):
    term = joined(product(stacked(green), (sigma[0, 0, 0], sigma[0, 0, 1])))
    real, imag = product_adjoint(term, (green[0, 0, 0], green[0, 0, 1]))
    out[0, 0] = real
    out[0, 1] = imag


def pair_kernel(own, green, sigma, out):
    term = joined(product(stacked(green), (sigma[0, 0, 0], sigma[0, 0, 1])))
    real, imag = product_adjoint(term, (green[0, 0, 0], green[0, 0, 1]))
    shape = out.shape[0], out.shape[3], out.shape[4]
    out[:, 0, 0] = (real + own[0, 0]).astype(BF16).reshape(shape)
    out[:, 0, 1] = (imag + own[0, 1]).astype(BF16).reshape(shape)


def final_kernel(screening, polar, out):
    size = out.shape[-1]
    parts = tuple(polar[:, 0, part].reshape(size, size) for part in range(2))
    left = joined(product(stacked(screening), parts))
    real, imag = product_adjoint(left, (screening[0, 0, 0], screening[0, 0, 1]))
    out[0, 0, 0] = real.astype(BF16)
    out[0, 0, 1] = imag.astype(BF16)


def correlate_kernel(forward, inverse_even, inverse_odd, early, late, out):
    count = out.shape[1]

    def spectrum(part):
        data = jnp.concatenate([early[part], late[part]], axis=0)
        return jnp.dot(forward[...], jnp.concatenate([data, data], axis=0), preferred_element_type=F32)

    real, imag = spectrum(0), spectrum(1)
    even_real, odd_real = real[:count], real[count:]
    even_imag, odd_imag = imag[:count], imag[count:]
    even = even_real * even_real + even_imag * even_imag
    odd = odd_real * odd_real + odd_imag * odd_imag
    cross = (even_real * odd_imag - even_imag * odd_real).astype(BF16)
    power = jnp.concatenate([even.astype(BF16), odd.astype(BF16)], axis=0)
    out[0] = jnp.dot(inverse_even[...], power, preferred_element_type=F32).astype(BF16)
    out[1] = jnp.dot(
        inverse_odd[...], jnp.concatenate([cross, cross], axis=0), preferred_element_type=F32
    ).astype(BF16)


def split_table(table):
    upper = table.astype(jnp.bfloat16)
    lower = (table - upper.astype(np.float64)).astype(jnp.bfloat16)
    return np.concatenate([upper, lower], axis=1)


def tables(energies, order):
    period = 2 * energies
    index = np.arange(energies)
    angle = 2.0 * math.pi / period * (np.outer(index, order) % period)
    even, odd = np.cos(angle), np.sin(angle)
    odd[0] = np.where(order % 2 == 0, 1.0, -1.0)
    forward = split_table(np.concatenate([even, odd], axis=0))
    angle = 2.0 * math.pi / period * (np.outer(index, index) % period)
    scale = 1.0 / (period * energies)
    cos_inv, sin_inv = 2.0 * scale * np.cos(angle), np.sin(angle)
    cos_inv[:, 0] = scale
    nyquist = cos_inv.copy()
    nyquist[:, 0] = scale * np.where(index % 2 == 0, 1.0, -1.0)
    inverse_even = np.concatenate([cos_inv, nyquist], axis=1).astype(jnp.bfloat16)
    inverse_odd = split_table(4.0 * scale * sin_inv)
    return forward, inverse_even, inverse_odd


def params(**more):
    return pltpu.CompilerParams(vmem_limit_bytes=20 * 2**20, **more)


def cost(flops, accessed):
    return pl.CostEstimate(flops=flops, bytes_accessed=accessed, transcendentals=0)


def block_spec(size, start=0):
    return pl.BlockSpec((1, 1, 2, size, size), lambda j: (0, j + start, 0, 0, 0))


def shards(green_diag, green_upper, sigma_lesser, screening):
    local, size = green_diag.shape[1], green_diag.shape[-1]
    devices = lax.axis_size("energy")
    energies = local * devices
    group = size // devices
    unit = 16 * size**3
    plane = 2 * size * size
    cuts = (0, FIRST, local)
    sigma_next = []
    for start, stop in zip(cuts, cuts[1:]):
        sigma_next.append(shifted(sigma_lesser[:, start:stop], "cuts", -1))
    own = pl.pallas_call(
        own_kernel,
        grid=(local,),
        in_specs=[block_spec(size), block_spec(size)],
        out_specs=pl.BlockSpec((1, 2, size, size), lambda j: (j, 0, 0, 0)),
        out_shape=jax.ShapeDtypeStruct((local, 2, size, size), F32),
        compiler_params=params(),
        cost_estimate=cost(local * unit, local * plane * 8),
        name="own",
    )(green_diag, sigma_lesser)

    pieces = []
    for index, (start, stop) in enumerate(zip(cuts, cuts[1:])):
        count = stop - start
        lesser = pl.pallas_call(
            pair_kernel,
            grid=(count,),
            in_specs=[
                pl.BlockSpec((1, 2, size, size), lambda j, start=start: (j + start, 0, 0, 0)),
                block_spec(size, start),
                block_spec(size),
            ],
            out_specs=pl.BlockSpec((devices, 1, 2, group, size), lambda j: (0, j, 0, 0, 0)),
            out_shape=jax.ShapeDtypeStruct((devices, count, 2, group, size), BF16),
            compiler_params=params(),
            cost_estimate=cost(count * unit, count * plane * 10),
        )(own, green_upper, sigma_next[index])
        piece = lax.all_to_all(lesser, "energy", split_axis=0, concat_axis=0, tiled=True)
        pieces.append(
            piece.transpose(2, 0, 1, 3, 4).reshape(2, devices * count, group * size)
        )

    grid = np.arange(energies).reshape(devices, local)
    order = np.concatenate([grid[:, a:b].reshape(-1) for a, b in zip(cuts, cuts[1:])])
    constants = [jnp.asarray(table) for table in tables(energies, order)]
    width = group * size
    step = width // 4
    polar = pl.pallas_call(
        correlate_kernel,
        grid=(width // step,),
        in_specs=[pl.BlockSpec(table.shape, lambda i: (0, 0)) for table in constants]
        + [pl.BlockSpec((2, piece.shape[1], step), lambda i: (0, 0, i)) for piece in pieces],
        out_specs=pl.BlockSpec((2, energies, step), lambda i: (0, 0, i)),
        out_shape=jax.ShapeDtypeStruct((2, energies, width), BF16),
        compiler_params=params(),
        cost_estimate=cost(2 * 2 * 256 * 256 * width * 2, energies * width * 8),
        name="correlate",
    )(*constants, *pieces)
    rows = polar.transpose(1, 0, 2).reshape(devices, local, 2, group, size)
    field = lax.all_to_all(rows, "energy", split_axis=0, concat_axis=0, tiled=True)

    return pl.pallas_call(
        final_kernel,
        grid=(local,),
        in_specs=[
            block_spec(size),
            pl.BlockSpec((devices, 1, 2, group, size), lambda j: (0, j, 0, 0, 0)),
        ],
        out_specs=block_spec(size),
        out_shape=jax.ShapeDtypeStruct(screening.shape, BF16),
        compiler_params=params(),
        cost_estimate=cost(local * unit, local * plane * 6),
        name="final",
    )(screening, field)


def solution(mesh):
    spec = P("cuts", "energy", None, None, None)
    return jax.shard_map(
        shards, mesh=mesh, in_specs=(spec, spec, spec, spec), out_specs=spec, check_vma=False
    )
```

```python
import functools
import math

import jax
import jax.numpy as jnp
import numpy as np
from jax import lax
from jax.experimental import pallas as pl
from jax.experimental.pallas import tpu as pltpu
from jax.sharding import PartitionSpec as P


F32 = jnp.float32
BF16 = jnp.bfloat16
CHUNK = 2


def shifted(value, axis, steps):
    count = lax.axis_size(axis)
    leading, last = (max(0, -steps), min(count, count - steps))
    return lax.ppermute(value, axis, [(source, source + steps) for source in range(leading, last)])


def product(left, right):
    rows = left.shape[0] // 2
    by_real = jnp.dot(left, right[0], preferred_element_type=F32)
    by_imag = jnp.dot(left, right[1], preferred_element_type=F32)
    return by_real[:rows] - by_imag[rows:], by_real[rows:] + by_imag[:rows]


def product_adjoint(left, right):
    rows = left.shape[0] // 2
    turned = functools.partial(
        lax.dot_general, dimension_numbers=(((1,), (1,)), ((), ())), preferred_element_type=F32
    )
    by_real = turned(left, right[0])
    by_imag = turned(left, right[1])
    return by_real[:rows] + by_imag[rows:], by_real[rows:] - by_imag[:rows]


def pair_of(ref, j):
    return ref[0, j, 0], ref[0, j, 1]


def joined(pair):
    return jnp.concatenate([part.astype(BF16) for part in pair], axis=0)


def halves(ref, j):
    rows = ref.shape[-2] // 2
    return [
        jnp.concatenate([ref[0, j, part, start : start + rows] for part in range(2)], axis=0)
        for start in (0, rows)
    ]


def sandwich(outer, inner):
    count = outer.shape[1]
    terms = [
        [joined(product(half, inner(j))) for half in halves(outer, j)] for j in range(count)
    ]
    return [[product_adjoint(term, pair_of(outer, j)) for term in terms[j]] for j in range(count)]


def own_kernel(green, sigma, out):
    rows = out.shape[-2] // 2
    for j, sides in enumerate(sandwich(green, lambda j: pair_of(sigma, j))):
        for side, parts in enumerate(sides):
            for part in range(2):
                out[j, part, side * rows : (side + 1) * rows] = parts[part]


def pair_kernel(own, green, sigma, out):
    devices, group, size = out.shape[0], out.shape[3], out.shape[4]
    rows, half = size // 2, devices // 2
    for j, sides in enumerate(sandwich(green, lambda j: pair_of(sigma, j))):
        for side, parts in enumerate(sides):
            for part in range(2):
                total = parts[part] + own[j, part, side * rows : (side + 1) * rows]
                out[side * half : (side + 1) * half, j, part] = total.astype(BF16).reshape(
                    half, group, size
                )


def final_kernel(screening, polar, out):
    size = out.shape[-1]
    rows = size // 2

    def inner(j):
        return tuple(polar[:, j, part].reshape(size, size) for part in range(2))

    for j, sides in enumerate(sandwich(screening, inner)):
        for side, parts in enumerate(sides):
            for part in range(2):
                out[0, j, part, side * rows : (side + 1) * rows] = parts[part].astype(BF16)


def correlate_kernel(forward, inverse_even, inverse_odd, early, late, out):
    count = out.shape[1]

    def spectrum(part):
        data = jnp.concatenate([early[part], late[part]], axis=0)
        return jnp.dot(forward[...], jnp.concatenate([data, data], axis=0), preferred_element_type=F32)

    real, imag = spectrum(0), spectrum(1)
    even_real, odd_real = real[:count], real[count:]
    even_imag, odd_imag = imag[:count], imag[count:]
    even = even_real * even_real + even_imag * even_imag
    odd = odd_real * odd_real + odd_imag * odd_imag
    cross = (even_real * odd_imag - even_imag * odd_real).astype(BF16)
    power = jnp.concatenate([even.astype(BF16), odd.astype(BF16)], axis=0)
    out[0] = jnp.dot(inverse_even[...], power, preferred_element_type=F32).astype(BF16)
    out[1] = jnp.dot(
        inverse_odd[...], jnp.concatenate([cross, cross], axis=0), preferred_element_type=F32
    ).astype(BF16)


def split_table(table):
    upper = table.astype(jnp.bfloat16)
    lower = (table - upper.astype(np.float64)).astype(jnp.bfloat16)
    return np.concatenate([upper, lower], axis=1)


def tables(energies, order):
    period = 2 * energies
    index = np.arange(energies)
    angle = 2.0 * math.pi / period * (np.outer(index, order) % period)
    even, odd = np.cos(angle), np.sin(angle)
    odd[0] = np.where(order % 2 == 0, 1.0, -1.0)
    forward = split_table(np.concatenate([even, odd], axis=0))
    angle = 2.0 * math.pi / period * (np.outer(index, index) % period)
    scale = 1.0 / (period * energies)
    cos_inv, sin_inv = 2.0 * scale * np.cos(angle), np.sin(angle)
    cos_inv[:, 0] = scale
    nyquist = cos_inv.copy()
    nyquist[:, 0] = scale * np.where(index % 2 == 0, 1.0, -1.0)
    inverse_even = np.concatenate([cos_inv, nyquist], axis=1).astype(jnp.bfloat16)
    inverse_odd = split_table(4.0 * scale * sin_inv)
    return forward, inverse_even, inverse_odd


def params(mebibytes=20):
    return pltpu.CompilerParams(vmem_limit_bytes=mebibytes * 2**20)


def cost(flops, accessed):
    return pl.CostEstimate(flops=flops, bytes_accessed=accessed, transcendentals=0)


def shards(green_diag, green_upper, sigma_lesser, screening):
    local, size = green_diag.shape[1], green_diag.shape[-1]
    devices = lax.axis_size("energy")
    energies = local * devices
    group = size // devices
    unit = 16 * size**3
    plane = 2 * size * size
    chunks = local // CHUNK
    blocks = (1, CHUNK, 2, size, size)

    def each(j):
        return (0, j, 0, 0, 0)

    def own_spec(start):
        return pl.BlockSpec((CHUNK, 2, size, size), lambda j: (j + start, 0, 0, 0))

    def rows_spec(start=0):
        return pl.BlockSpec((devices, CHUNK, 2, group, size), lambda j: (0, j + start, 0, 0, 0))

    sigma_next = []
    for index in range(chunks):
        part = sigma_lesser[:, index * CHUNK : (index + 1) * CHUNK]
        sigma_next.append(shifted(part, "cuts", -1))
    own = pl.pallas_call(
        own_kernel,
        grid=(chunks,),
        in_specs=[pl.BlockSpec(blocks, each)] * 2,
        out_specs=own_spec(0),
        out_shape=jax.ShapeDtypeStruct((local, 2, size, size), F32),
        compiler_params=params(),
        cost_estimate=cost(local * unit, local * plane * 8),
        name="own",
    )(green_diag, sigma_lesser)

    pieces = []
    for index in range(chunks):
        lesser = pl.pallas_call(
            pair_kernel,
            grid=(1,),
            in_specs=[
                own_spec(index),
                pl.BlockSpec(blocks, lambda j, index=index: (0, j + index, 0, 0, 0)),
                pl.BlockSpec(blocks, each),
            ],
            out_specs=rows_spec(),
            out_shape=pltpu.HBM((devices, CHUNK, 2, group, size), BF16),
            compiler_params=params(),
            cost_estimate=cost(CHUNK * unit, CHUNK * plane * 10),
        )(own, green_upper, sigma_next[index])
        piece = lax.all_to_all(lesser, "energy", split_axis=0, concat_axis=0, tiled=True)
        pieces.append(
            piece.transpose(2, 0, 1, 3, 4).reshape(2, devices * CHUNK, group * size)
        )

    grid = np.arange(energies).reshape(devices, chunks, CHUNK)
    order = grid.transpose(1, 0, 2).reshape(-1)
    constants = [jnp.asarray(table) for table in tables(energies, order)]
    width = group * size
    step = width // 2
    polar = pl.pallas_call(
        correlate_kernel,
        grid=(width // step,),
        in_specs=[pl.BlockSpec(table.shape, lambda i: (0, 0)) for table in constants]
        + [pl.BlockSpec((2, piece.shape[1], step), lambda i: (0, 0, i)) for piece in pieces],
        out_specs=pl.BlockSpec((2, energies, step), lambda i: (0, 0, i)),
        out_shape=jax.ShapeDtypeStruct((2, energies, width), BF16),
        compiler_params=params(),
        cost_estimate=cost(2 * 2 * 256 * 256 * width * 2, energies * width * 8),
        name="correlate",
    )(*constants, *pieces)
    rows = polar.transpose(1, 0, 2).reshape(devices, local, 2, group, size)
    field = lax.all_to_all(rows, "energy", split_axis=0, concat_axis=0, tiled=True)

    return pl.pallas_call(
        final_kernel,
        grid=(chunks,),
        in_specs=[pl.BlockSpec(blocks, each), rows_spec()],
        out_specs=pl.BlockSpec(blocks, each),
        out_shape=jax.ShapeDtypeStruct(screening.shape, BF16),
        compiler_params=params(),
        cost_estimate=cost(local * unit, local * plane * 6),
        name="final",
    )(screening, field)


def solution(mesh):
    spec = P("cuts", "energy", None, None, None)
    return jax.shard_map(
        shards, mesh=mesh, in_specs=(spec, spec, spec, spec), out_specs=spec, check_vma=False
    )
```

```python
import functools
import math

import jax
import jax.numpy as jnp
import numpy as np
from jax import lax
from jax.experimental import pallas as pl
from jax.experimental.pallas import tpu as pltpu
from jax.sharding import PartitionSpec as P

F32 = jnp.float32
BF16 = jnp.bfloat16
CHUNK = 2


def shifted(value, axis, steps):
    count = lax.axis_size(axis)
    leading, last = (max(0, -steps), min(count, count - steps))
    return lax.ppermute(value, axis, [(source, source + steps) for source in range(leading, last)])


def product(left, right):
    rows = left.shape[0] // 2
    by_real = jnp.dot(left, right[0], preferred_element_type=F32)
    by_imag = jnp.dot(left, right[1], preferred_element_type=F32)
    return by_real[:rows] - by_imag[rows:], by_real[rows:] + by_imag[:rows]


def product_adjoint(left, right):
    rows = left.shape[0] // 2
    turned = functools.partial(
        lax.dot_general, dimension_numbers=(((1,), (1,)), ((), ())), preferred_element_type=F32
    )
    by_real = turned(left, right[0])
    by_imag = turned(left, right[1])
    return by_real[:rows] + by_imag[rows:], by_real[rows:] - by_imag[:rows]


def pair_of(ref, j):
    return ref[0, j, 0], ref[0, j, 1]


def joined(pair):
    return jnp.concatenate([part.astype(BF16) for part in pair], axis=0)


def halves(ref, j):
    rows = ref.shape[-2] // 2
    return [
        jnp.concatenate([ref[0, j, part, start : start + rows] for part in range(2)], axis=0)
        for start in (0, rows)
    ]


def sandwich(outer, inner):
    count = outer.shape[1]
    terms = [
        [joined(product(half, inner(j))) for half in halves(outer, j)] for j in range(count)
    ]
    return [[product_adjoint(term, pair_of(outer, j)) for term in terms[j]] for j in range(count)]


def own_kernel(green, sigma, out):
    rows = out.shape[-2] // 2
    for j, sides in enumerate(sandwich(green, lambda j: pair_of(sigma, j))):
        for side, parts in enumerate(sides):
            for part in range(2):
                out[j, part, side * rows : (side + 1) * rows] = parts[part]


def pair_kernel(own, green, sigma, out):
    devices, group, size = out.shape[0], out.shape[3], out.shape[4]
    rows, half = size // 2, devices // 2
    for j, sides in enumerate(sandwich(green, lambda j: pair_of(sigma, j))):
        for side, parts in enumerate(sides):
            for part in range(2):
                total = parts[part] + own[j, part, side * rows : (side + 1) * rows]
                out[side * half : (side + 1) * half, j, part] = total.astype(BF16).reshape(
                    half, group, size
                )


def final_kernel(screening, polar, out):
    size = out.shape[-1]
    rows = size // 2

    def inner(j):
        return tuple(polar[:, j, part].reshape(size, size) for part in range(2))

    for j, sides in enumerate(sandwich(screening, inner)):
        for side, parts in enumerate(sides):
            for part in range(2):
                out[0, j, part, side * rows : (side + 1) * rows] = parts[part].astype(BF16)


def correlate_kernel(forward, inverse_even, inverse_odd, entries, out):
    count = out.shape[1]

    def spectrum(part):
        data = entries[part]
        return jnp.dot(forward[...], jnp.concatenate([data, data], axis=0), preferred_element_type=F32)

    real, imag = spectrum(0), spectrum(1)
    even_real, odd_real = real[:count], real[count:]
    even_imag, odd_imag = imag[:count], imag[count:]
    even = even_real * even_real + even_imag * even_imag
    odd = odd_real * odd_real + odd_imag * odd_imag
    cross = (even_real * odd_imag - even_imag * odd_real).astype(BF16)
    power = jnp.concatenate([even.astype(BF16), odd.astype(BF16)], axis=0)
    out[0] = jnp.dot(inverse_even[...], power, preferred_element_type=F32).astype(BF16)
    out[1] = jnp.dot(
        inverse_odd[...], jnp.concatenate([cross, cross], axis=0), preferred_element_type=F32
    ).astype(BF16)


def split_table(table):
    upper = table.astype(jnp.bfloat16)
    lower = (table - upper.astype(np.float64)).astype(jnp.bfloat16)
    return np.concatenate([upper, lower], axis=1)


def tables(energies):
    period = 2 * energies
    index = np.arange(energies)
    angle = 2.0 * math.pi / period * (np.outer(index, index) % period)
    even, odd = np.cos(angle), np.sin(angle)
    odd[0] = np.where(index % 2 == 0, 1.0, -1.0)
    forward = split_table(np.concatenate([even, odd], axis=0))
    scale = 1.0 / (period * energies)
    cos_inv, sin_inv = 2.0 * scale * np.cos(angle), np.sin(angle)
    cos_inv[:, 0] = scale
    nyquist = cos_inv.copy()
    nyquist[:, 0] = scale * np.where(index % 2 == 0, 1.0, -1.0)
    inverse_even = np.concatenate([cos_inv, nyquist], axis=1).astype(jnp.bfloat16)
    inverse_odd = split_table(4.0 * scale * sin_inv)
    return forward, inverse_even, inverse_odd


def params(mebibytes=20):
    return pltpu.CompilerParams(vmem_limit_bytes=mebibytes * 2**20)


def cost(flops, accessed):
    return pl.CostEstimate(flops=flops, bytes_accessed=accessed, transcendentals=0)


def shards(green_diag, green_upper, sigma_lesser, screening):
    local, size = green_diag.shape[1], green_diag.shape[-1]
    devices = lax.axis_size("energy")
    energies = local * devices
    group = size // devices
    unit = 16 * size**3
    plane = 2 * size * size
    chunks = local // CHUNK
    blocks = (1, CHUNK, 2, size, size)

    def each(j):
        return (0, j, 0, 0, 0)

    def own_spec(start):
        return pl.BlockSpec((CHUNK, 2, size, size), lambda j: (j + start, 0, 0, 0))

    def rows_spec(start=0):
        return pl.BlockSpec((devices, CHUNK, 2, group, size), lambda j: (0, j + start, 0, 0, 0))

    sigma_next = shifted(sigma_lesser, "cuts", -1)
    own = pl.pallas_call(
        own_kernel,
        grid=(chunks,),
        in_specs=[pl.BlockSpec(blocks, each)] * 2,
        out_specs=own_spec(0),
        out_shape=jax.ShapeDtypeStruct((local, 2, size, size), F32),
        compiler_params=params(),
        cost_estimate=cost(local * unit, local * plane * 8),
        name="own",
    )(green_diag, sigma_lesser)
    lesser = pl.pallas_call(
        pair_kernel,
        grid=(chunks,),
        in_specs=[own_spec(0), pl.BlockSpec(blocks, each), pl.BlockSpec(blocks, each)],
        out_specs=rows_spec(),
        out_shape=jax.ShapeDtypeStruct((devices, local, 2, group, size), BF16),
        compiler_params=params(),
        cost_estimate=cost(local * unit, local * plane * 10),
        name="pair",
    )(own, green_upper, sigma_next)
    entries = lax.all_to_all(lesser, "energy", split_axis=0, concat_axis=0, tiled=True)
    entries = entries.transpose(2, 0, 1, 3, 4).reshape(2, energies, group * size)
    constants = [jnp.asarray(table) for table in tables(energies)]
    width = group * size
    step = width // 2
    polar = pl.pallas_call(
        correlate_kernel,
        grid=(width // step,),
        in_specs=[pl.BlockSpec(table.shape, lambda i: (0, 0)) for table in constants]
        + [pl.BlockSpec((2, energies, step), lambda i: (0, 0, i))],
        out_specs=pl.BlockSpec((2, energies, step), lambda i: (0, 0, i)),
        out_shape=jax.ShapeDtypeStruct((2, energies, width), BF16),
        compiler_params=params(),
        cost_estimate=cost(2 * 2 * 256 * 256 * width * 2, energies * width * 8),
        name="correlate",
    )(*constants, entries)
    rows = polar.transpose(1, 0, 2).reshape(devices, local, 2, group, size)
    field = lax.all_to_all(rows, "energy", split_axis=0, concat_axis=0, tiled=True)

    return pl.pallas_call(
        final_kernel,
        grid=(chunks,),
        in_specs=[pl.BlockSpec(blocks, each), rows_spec()],
        out_specs=pl.BlockSpec(blocks, each),
        out_shape=jax.ShapeDtypeStruct(screening.shape, BF16),
        compiler_params=params(),
        cost_estimate=cost(local * unit, local * plane * 6),
        name="final",
    )(screening, field)


def solution(mesh):
    spec = P("cuts", "energy", None, None, None)
    return jax.shard_map(
        shards, mesh=mesh, in_specs=(spec, spec, spec, spec), out_specs=spec, check_vma=False
    )
```

```python
import functools
import math

import jax
import jax.numpy as jnp
import numpy as np
from jax import lax
from jax.experimental import pallas as pl
from jax.experimental.pallas import tpu as pltpu
from jax.sharding import PartitionSpec as P

F32 = jnp.float32
BF16 = jnp.bfloat16
CHUNK = 2


def shifted(value, axis, steps):
    count = lax.axis_size(axis)
    leading, last = (max(0, -steps), min(count, count - steps))
    return lax.ppermute(value, axis, [(source, source + steps) for source in range(leading, last)])


def product(left, right):
    rows = left.shape[0] // 2
    by_real = jnp.dot(left, right[0], preferred_element_type=F32)
    by_imag = jnp.dot(left, right[1], preferred_element_type=F32)
    return by_real[:rows] - by_imag[rows:], by_real[rows:] + by_imag[:rows]


def product_adjoint(left, right):
    rows = left.shape[0] // 2
    turned = functools.partial(
        lax.dot_general, dimension_numbers=(((1,), (1,)), ((), ())), preferred_element_type=F32
    )
    by_real = turned(left, right[0])
    by_imag = turned(left, right[1])
    return by_real[:rows] + by_imag[rows:], by_real[rows:] - by_imag[:rows]


def pair_of(ref, j):
    return ref[0, j, 0], ref[0, j, 1]


def joined(pair):
    return jnp.concatenate([part.astype(BF16) for part in pair], axis=0)


def halves(ref, j):
    rows = ref.shape[-2] // 2
    return [
        jnp.concatenate([ref[0, j, part, start : start + rows] for part in range(2)], axis=0)
        for start in (0, rows)
    ]


def sandwich(outer, inner):
    count = outer.shape[1]
    terms = [
        [joined(product(half, inner(j))) for half in halves(outer, j)] for j in range(count)
    ]
    return [[product_adjoint(term, pair_of(outer, j)) for term in terms[j]] for j in range(count)]


def own_kernel(green, sigma, out):
    rows = out.shape[-2] // 2
    for j, sides in enumerate(sandwich(green, lambda j: pair_of(sigma, j))):
        for side, parts in enumerate(sides):
            for part in range(2):
                out[j, part, side * rows : (side + 1) * rows] = parts[part]


def pair_kernel(own, green, sigma, out):
    devices, group, size = out.shape[0], out.shape[3], out.shape[4]
    rows, half = size // 2, devices // 2
    for j, sides in enumerate(sandwich(green, lambda j: pair_of(sigma, j))):
        for side, parts in enumerate(sides):
            for part in range(2):
                total = parts[part] + own[j, part, side * rows : (side + 1) * rows]
                out[side * half : (side + 1) * half, j, part] = total.astype(BF16).reshape(
                    half, group, size
                )


def final_kernel(screening, polar, out):
    size = out.shape[-1]
    rows = size // 2

    def inner(j):
        return tuple(polar[:, j, part].reshape(size, size) for part in range(2))

    for j, sides in enumerate(sandwich(screening, inner)):
        for side, parts in enumerate(sides):
            for part in range(2):
                out[0, j, part, side * rows : (side + 1) * rows] = parts[part].astype(BF16)


def correlate_kernel(forward, inverse_even, inverse_odd, reals, imags, out):
    count = out.shape[1]

    def spectrum(part):
        data = part[...]
        return jnp.dot(forward[...], jnp.concatenate([data, data], axis=0), preferred_element_type=F32)

    real, imag = spectrum(reals), spectrum(imags)
    even_real, odd_real = real[:count], real[count:]
    even_imag, odd_imag = imag[:count], imag[count:]
    even = even_real * even_real + even_imag * even_imag
    odd = odd_real * odd_real + odd_imag * odd_imag
    cross = (even_real * odd_imag - even_imag * odd_real).astype(BF16)
    power = jnp.concatenate([even.astype(BF16), odd.astype(BF16)], axis=0)
    out[0] = jnp.dot(inverse_even[...], power, preferred_element_type=F32).astype(BF16)
    out[1] = jnp.dot(
        inverse_odd[...], jnp.concatenate([cross, cross], axis=0), preferred_element_type=F32
    ).astype(BF16)


def split_table(table):
    upper = table.astype(jnp.bfloat16)
    lower = (table - upper.astype(np.float64)).astype(jnp.bfloat16)
    return np.concatenate([upper, lower], axis=1)


def tables(energies):
    period = 2 * energies
    index = np.arange(energies)
    angle = 2.0 * math.pi / period * (np.outer(index, index) % period)
    even, odd = np.cos(angle), np.sin(angle)
    odd[0] = np.where(index % 2 == 0, 1.0, -1.0)
    forward = split_table(np.concatenate([even, odd], axis=0))
    scale = 1.0 / (period * energies)
    cos_inv, sin_inv = 2.0 * scale * np.cos(angle), np.sin(angle)
    cos_inv[:, 0] = scale
    nyquist = cos_inv.copy()
    nyquist[:, 0] = scale * np.where(index % 2 == 0, 1.0, -1.0)
    inverse_even = np.concatenate([cos_inv, nyquist], axis=1).astype(jnp.bfloat16)
    inverse_odd = split_table(4.0 * scale * sin_inv)
    return forward, inverse_even, inverse_odd


def params(mebibytes=20):
    return pltpu.CompilerParams(vmem_limit_bytes=mebibytes * 2**20)


def cost(flops, accessed):
    return pl.CostEstimate(flops=flops, bytes_accessed=accessed, transcendentals=0)


def shards(green_diag, green_upper, sigma_lesser, screening):
    local, size = green_diag.shape[1], green_diag.shape[-1]
    devices = lax.axis_size("energy")
    energies = local * devices
    group = size // devices
    unit = 16 * size**3
    plane = 2 * size * size
    chunks = local // CHUNK
    blocks = (1, CHUNK, 2, size, size)

    def each(j):
        return (0, j, 0, 0, 0)

    def own_spec(start):
        return pl.BlockSpec((CHUNK, 2, size, size), lambda j: (j + start, 0, 0, 0))

    def rows_spec(start=0):
        return pl.BlockSpec((devices, CHUNK, 2, group, size), lambda j: (0, j + start, 0, 0, 0))

    sigma_next = shifted(sigma_lesser, "cuts", -1)
    own = pl.pallas_call(
        own_kernel,
        grid=(chunks,),
        in_specs=[pl.BlockSpec(blocks, each)] * 2,
        out_specs=own_spec(0),
        out_shape=jax.ShapeDtypeStruct((local, 2, size, size), F32),
        compiler_params=params(),
        cost_estimate=cost(local * unit, local * plane * 8),
        name="own",
    )(green_diag, sigma_lesser)
    lesser = pl.pallas_call(
        pair_kernel,
        grid=(chunks,),
        in_specs=[own_spec(0), pl.BlockSpec(blocks, each), pl.BlockSpec(blocks, each)],
        out_specs=rows_spec(),
        out_shape=jax.ShapeDtypeStruct((devices, local, 2, group, size), BF16),
        compiler_params=params(),
        cost_estimate=cost(local * unit, local * plane * 10),
        name="pair",
    )(own, green_upper, sigma_next)
    entries = lax.all_to_all(lesser, "energy", split_axis=0, concat_axis=0, tiled=True)
    entries = entries.reshape(energies, 2 * group * size)
    constants = [jnp.asarray(table) for table in tables(energies)]
    width = group * size
    step = width // 2
    polar = pl.pallas_call(
        correlate_kernel,
        grid=(width // step,),
        in_specs=[pl.BlockSpec(table.shape, lambda i: (0, 0)) for table in constants]
        + [
            pl.BlockSpec((energies, step), lambda i: (0, i)),
            pl.BlockSpec((energies, step), lambda i: (0, i + width // step)),
        ],
        out_specs=pl.BlockSpec((2, energies, step), lambda i: (0, 0, i)),
        out_shape=jax.ShapeDtypeStruct((2, energies, width), BF16),
        compiler_params=params(),
        cost_estimate=cost(2 * 2 * 256 * 256 * width * 2, energies * width * 8),
        name="correlate",
    )(*constants, entries, entries)
    rows = polar.transpose(1, 0, 2).reshape(devices, local, 2, group, size)
    field = lax.all_to_all(rows, "energy", split_axis=0, concat_axis=0, tiled=True)

    return pl.pallas_call(
        final_kernel,
        grid=(chunks,),
        in_specs=[pl.BlockSpec(blocks, each), rows_spec()],
        out_specs=pl.BlockSpec(blocks, each),
        out_shape=jax.ShapeDtypeStruct(screening.shape, BF16),
        compiler_params=params(),
        cost_estimate=cost(local * unit, local * plane * 6),
        name="final",
    )(screening, field)


def solution(mesh):
    spec = P("cuts", "energy", None, None, None)
    return jax.shard_map(
        shards, mesh=mesh, in_specs=(spec, spec, spec, spec), out_specs=spec, check_vma=False
    )
```

```python
import functools
import math

import jax
import jax.numpy as jnp
import numpy as np
from jax import lax
from jax.experimental import pallas as pl
from jax.experimental.pallas import tpu as pltpu
from jax.sharding import PartitionSpec as P


F32 = jnp.float32
BF16 = jnp.bfloat16
FIRST, MIDDLE = 1, 3


def moved(value, pairs):
    return lax.ppermute(value, "cuts", pairs)


def product(left, right):
    rows = left.shape[0] // 2
    by_real = jnp.dot(left, right[0], preferred_element_type=F32)
    by_imag = jnp.dot(left, right[1], preferred_element_type=F32)
    return by_real[:rows] - by_imag[rows:], by_real[rows:] + by_imag[:rows]


def product_adjoint(left, right):
    rows = left.shape[0] // 2
    turned = functools.partial(
        lax.dot_general, dimension_numbers=(((1,), (1,)), ((), ())), preferred_element_type=F32
    )
    by_real = turned(left, right[0])
    by_imag = turned(left, right[1])
    return by_real[:rows] + by_imag[rows:], by_real[rows:] - by_imag[:rows]


def pair_of(ref, j):
    return ref[0, j, 0], ref[0, j, 1]


def joined(pair):
    return jnp.concatenate([part.astype(BF16) for part in pair], axis=0)


def halves(ref, j):
    rows = ref.shape[-2] // 2
    return [
        jnp.concatenate([ref[0, j, part, start : start + rows] for part in range(2)], axis=0)
        for start in (0, rows)
    ]


def sandwich(outer, inner):
    count = outer.shape[1]
    terms = [
        [joined(product(half, inner(j))) for half in halves(outer, j)] for j in range(count)
    ]
    return [[product_adjoint(term, pair_of(outer, j)) for term in terms[j]] for j in range(count)]


def own_kernel(green, sigma, out):
    rows = out.shape[-2] // 2
    (sides,) = sandwich(green, lambda j: pair_of(sigma, j))
    for side, parts in enumerate(sides):
        for part in range(2):
            out[0, part, side * rows : (side + 1) * rows] = parts[part]


def store_lesser(own, green, sigma, out):
    devices, group, size = out.shape[0], out.shape[3], out.shape[4]
    rows, half = size // 2, devices // 2
    (sides,) = sandwich(green, lambda j: sigma)
    for side, parts in enumerate(sides):
        for part in range(2):
            total = parts[part] + own[0, part, side * rows : (side + 1) * rows]
            out[side * half : (side + 1) * half, 0, part] = total.astype(BF16).reshape(half, group, size)


def plain_kernel(own, green, sigma, out):
    store_lesser(own, green, pair_of(sigma, 0), out)


def last_kernel(own, green, within, crossed, _, out):
    sigma = tuple(within[0, 0, part] + crossed[0, 0, part] for part in range(2))
    store_lesser(own, green, sigma, out)


def final_kernel(screening, polar, out):
    size = out.shape[-1]
    rows = size // 2

    def inner(j):
        return tuple(polar[:, j, part].reshape(size, size) for part in range(2))

    for j, sides in enumerate(sandwich(screening, inner)):
        for side, parts in enumerate(sides):
            for part in range(2):
                out[0, j, part, side * rows : (side + 1) * rows] = parts[part].astype(BF16)


def correlate_kernel(forward, inverse_even, inverse_odd, *rest):
    *parts, out = rest
    count = out.shape[1]

    def spectrum(early, late):
        data = jnp.concatenate([early[...], late[...]], axis=0)
        return jnp.dot(forward[...], jnp.concatenate([data, data], axis=0), preferred_element_type=F32)

    real, imag = spectrum(*parts[:2]), spectrum(*parts[2:])
    even_real, odd_real = real[:count], real[count:]
    even_imag, odd_imag = imag[:count], imag[count:]
    even = even_real * even_real + even_imag * even_imag
    odd = odd_real * odd_real + odd_imag * odd_imag
    cross = (even_real * odd_imag - even_imag * odd_real).astype(BF16)
    power = jnp.concatenate([even.astype(BF16), odd.astype(BF16)], axis=0)
    out[0] = jnp.dot(inverse_even[...], power, preferred_element_type=F32).astype(BF16)
    out[1] = jnp.dot(
        inverse_odd[...], jnp.concatenate([cross, cross], axis=0), preferred_element_type=F32
    ).astype(BF16)


def split_table(table):
    upper = table.astype(jnp.bfloat16)
    lower = (table - upper.astype(np.float64)).astype(jnp.bfloat16)
    return np.concatenate([upper, lower], axis=1)


def tables(energies, order):
    period = 2 * energies
    index = np.arange(energies)
    angle = 2.0 * math.pi / period * (np.outer(index, order) % period)
    even, odd = np.cos(angle), np.sin(angle)
    odd[0] = np.where(order % 2 == 0, 1.0, -1.0)
    forward = split_table(np.concatenate([even, odd], axis=0))
    angle = 2.0 * math.pi / period * (np.outer(index, index) % period)
    scale = 1.0 / (period * energies)
    cos_inv, sin_inv = 2.0 * scale * np.cos(angle), np.sin(angle)
    cos_inv[:, 0] = scale
    nyquist = cos_inv.copy()
    nyquist[:, 0] = scale * np.where(index % 2 == 0, 1.0, -1.0)
    inverse_even = np.concatenate([cos_inv, nyquist], axis=1).astype(jnp.bfloat16)
    inverse_odd = split_table(4.0 * scale * sin_inv)
    return forward, inverse_even, inverse_odd


def params(mebibytes=20):
    return pltpu.CompilerParams(vmem_limit_bytes=mebibytes * 2**20)


def cost(flops, accessed):
    return pl.CostEstimate(flops=flops, bytes_accessed=accessed, transcendentals=0)


def shards(green_diag, green_upper, sigma_lesser, screening):
    local, size = green_diag.shape[1], green_diag.shape[-1]
    devices, cuts = lax.axis_size("energy"), lax.axis_size("cuts")
    energies = local * devices
    group = size // devices
    unit = 16 * size**3
    plane = 2 * size * size
    one = (1, 1, 2, size, size)
    single = (1, 2, size, size)

    def energy(start=0):
        return pl.BlockSpec(one, lambda j: (0, j + start, 0, 0, 0))

    half = cuts // 2
    direct = [(s + 1, s) for s in range(cuts - 1)]
    across = (half, half - 1)
    within = [pair for pair in direct if pair != across]
    next_first = moved(sigma_lesser[:, :FIRST], direct)
    next_middle = moved(sigma_lesser[:, FIRST:MIDDLE], direct)
    sigma_last = lax.optimization_barrier(sigma_lesser)[:, MIDDLE:]
    next_last = moved(sigma_last, within)
    crossed = moved(sigma_last, [across])

    def own_of(start, stop):
        return pl.pallas_call(
            own_kernel,
            grid=(stop - start,),
            in_specs=[energy(start), energy(start)],
            out_specs=pl.BlockSpec(single, lambda j: (j, 0, 0, 0)),
            out_shape=jax.ShapeDtypeStruct((stop - start, 2, size, size), F32),
            compiler_params=params(),
            cost_estimate=cost((stop - start) * unit, (stop - start) * plane * 8),
        )(*(pltpu.with_memory_space_constraint(a, pltpu.HBM) for a in (green_diag, sigma_lesser)))

    own_first = own_of(0, FIRST)
    own_rest = own_of(FIRST, local)

    def lesser_of(kernel, own, start, stop, into, sigmas, buffer=None):
        count = stop - start
        base = start if own is own_first else start - FIRST
        whole = [] if buffer is None else [buffer]
        total = FIRST if own is own_first else local - FIRST
        return pl.pallas_call(
            kernel,
            grid=(count,),
            in_specs=[pl.BlockSpec(single, lambda j: (j + base, 0, 0, 0)), energy(start)]
            + [energy()] * len(sigmas)
            + [pl.BlockSpec(memory_space=pl.ANY)] * len(whole),
            out_specs=pl.BlockSpec((devices, 1, 2, group, size), lambda j: (0, j + into, 0, 0, 0)),
            out_shape=pltpu.HBM((devices, total, 2, group, size), BF16),
            input_output_aliases={2 + len(sigmas): 0} if whole else {},
            compiler_params=params(),
            cost_estimate=cost(count * unit, count * plane * 10),
        )(own, green_upper, *sigmas, *whole)

    def exchanged(value):
        return lax.all_to_all(value, "energy", split_axis=0, concat_axis=0, tiled=True)

    early = exchanged(lesser_of(plain_kernel, own_first, 0, FIRST, 0, [next_first]))
    rest = lesser_of(plain_kernel, own_rest, FIRST, MIDDLE, 0, [next_middle])
    sigmas = [next_last, crossed]
    rest = lesser_of(last_kernel, own_rest, MIDDLE, local, MIDDLE - FIRST, sigmas, rest)
    late = exchanged(rest)
    pieces = [piece.reshape(-1, 2 * group * size) for piece in (early, late)]

    grid = np.arange(energies).reshape(devices, local)
    order = np.concatenate([grid[:, :FIRST].reshape(-1), grid[:, FIRST:].reshape(-1)])
    constants = [jnp.asarray(table) for table in tables(energies, order)]
    width = group * size
    step = width // 2
    polar = pl.pallas_call(
        correlate_kernel,
        grid=(width // step,),
        in_specs=[pl.BlockSpec(table.shape, lambda i: (0, 0)) for table in constants]
        + [
            pl.BlockSpec((piece.shape[0], step), lambda i, start=start: (0, i + start))
            for start in (0, width // step)
            for piece in pieces
        ],
        out_specs=pl.BlockSpec((2, energies, step), lambda i: (0, 0, i)),
        out_shape=jax.ShapeDtypeStruct((2, energies, width), BF16),
        compiler_params=params(),
        cost_estimate=cost(2 * 2 * 256 * 256 * width * 2, energies * width * 8),
        name="correlate",
    )(*constants, *pieces, *pieces)
    field = exchanged(polar.transpose(1, 0, 2).reshape(devices, local, 2, group, size))

    pair = 2
    return pl.pallas_call(
        final_kernel,
        grid=(local // pair,),
        in_specs=[
            pl.BlockSpec((1, pair, 2, size, size), lambda j: (0, j, 0, 0, 0)),
            pl.BlockSpec((devices, pair, 2, group, size), lambda j: (0, j, 0, 0, 0)),
        ],
        out_specs=pl.BlockSpec((1, pair, 2, size, size), lambda j: (0, j, 0, 0, 0)),
        out_shape=jax.ShapeDtypeStruct(screening.shape, BF16),
        compiler_params=params(),
        cost_estimate=cost(local * unit, local * plane * 6),
        name="final",
    )(screening, field)


def solution(mesh):
    spec = P("cuts", "energy", None, None, None)
    return jax.shard_map(
        shards, mesh=mesh, in_specs=(spec, spec, spec, spec), out_specs=spec, check_vma=False
    )
```
